128 devices in a mesh: row: 8 (over x, z_hi), col: 16 (over z_lo, y, core).
Axes of the slice: x: 4, y: 4, z: 4 (z_hi: 2, z_lo: 2; z = z_hi * 2 + z_lo), core: 2. Of those that a mesh axis runs over, the one named last changes fastest.
Arguments:
- amplitudes: bfloat16 [800, 800, 768], P('row', 'col'), may hold values from -6 to 6
- integrals: bfloat16 [800, 800, 1024], P('row', 'col'), may hold values from -0.1875 to 0.1875
- window_index: int32 [1024], replicated, may hold values from 0 to 639999, as said below
Outputs:
- residual: bfloat16 [800, 800, 768], P('row', 'col')
- pair_energy: float32 [768], replicated
The draws below stay inside these ranges and needn't reach their ends.
Inputs may be any that keep to these rules, and one draw needn't show every extreme that they name: `window_index`: the window pairs are distinct; pair k lies in the block of a rows and b columns owned by device number k // 8 in row-major order of the (a, b) device grid, 8 pairs for each block.
All inputs are finite; a program needn't handle non-finite values.
Results may differ from the reference program's by a relative error of at most 0.001.
Values may be sent and summed in bfloat16 or wider, within the bound.
No kernel may reach another device: no remote copies, remote signals or barrier semaphores. Data moves between devices by JAX's collectives and lax.ppermute only.
A program may use at most 128 MiB of HBM per device.

```python
import jax
import jax.numpy as jnp
from jax import lax

VIRT = 800
PAIRS = 768
KD = 8
WINDOW = 1024
N_ROW = 8
N_COL = 16


def draw_window_index(key, part):
    block_rows = VIRT // N_ROW
    block_cols = VIRT // N_COL
    device_keys = jax.random.split(jax.random.fold_in(key, 17), N_ROW * N_COL)

    def choose_cells(one_key):
        return jax.random.permutation(one_key, block_rows * block_cols)[:KD].astype(jnp.int32)
    picked = jax.vmap(choose_cells)(device_keys)
    device_ids = jnp.arange(N_ROW * N_COL, dtype=jnp.int32)
    row_ids = device_ids // N_COL
    col_ids = device_ids % N_COL
    a_index = row_ids[:, None] * block_rows + picked // block_cols
    b_index = col_ids[:, None] * block_cols + picked % block_cols
    return (a_index * VIRT + b_index).reshape(-1).astype(jnp.int32)


def level_of(stream_key, extent, pieces, least, high):
    level = 1.0
    for dim, blocks in pieces:
        draws = jax.random.uniform(jax.random.fold_in(jax.random.fold_in(stream_key, 6), dim), (blocks,), jnp.float32, least / len(pieces), high / len(pieces))
        level = level * jnp.repeat(jnp.exp(draws), extent[dim] // blocks).reshape((-1,) + (1,) * (len(extent) - 1 - dim))
    return level


def gaussian(key, shape, width, most, pieces=(), kind=jnp.bfloat16):
    entries = jax.random.normal(key, shape, jnp.float32) * width
    if len(pieces) > 0:
        entries = level_of(key, shape, pieces, -0.22, 0.18) * entries
    return jnp.clip(entries, min=-most, max=most).astype(kind)


def setup_inputs(seed: int = 0) -> dict:
    seeds = jax.random.split(jax.random.key(seed), 4)
    amplitudes = gaussian(seeds[0], (VIRT, VIRT, PAIRS), 1.0, 6.0, ((0, 8), (1, 16)))
    integrals = gaussian(seeds[1], (VIRT, VIRT, WINDOW), WINDOW ** -0.5, 0.1875, ((0, 8), (1, 16)))
    window_index = draw_window_index(jax.random.fold_in(seeds[3], 71), 0)
    return dict(amplitudes=amplitudes, integrals=integrals, window_index=window_index)


def reference(amplitudes, integrals, window_index):
    flattened = amplitudes.reshape(VIRT * VIRT, PAIRS)
    columns = jnp.take(flattened, window_index, axis=0)
    block_rows = VIRT // N_ROW

    def one_block(block_index):
        start = (block_index * block_rows).astype(jnp.int32)
        part_ints = lax.dynamic_slice_in_dim(integrals, start, block_rows, 0)
        part_amps = lax.dynamic_slice_in_dim(amplitudes, start, block_rows, 0)
        full = jnp.dot(part_ints.reshape(block_rows * VIRT, WINDOW), columns, preferred_element_type=jnp.float32)
        energy = jnp.sum(part_amps.reshape(block_rows * VIRT, PAIRS).astype(jnp.float32) * full, axis=0)
        return full.astype(jnp.bfloat16), energy

    blocks, energies = lax.map(one_block, jnp.arange(N_ROW, dtype=jnp.int32))
    residual = blocks.reshape(VIRT, VIRT, PAIRS)
    pair_energy = jnp.sum(energies, axis=0) / VIRT
    return residual, pair_energy
```

```python
import functools

import jax
import jax.numpy as jnp
from jax import lax
from jax.experimental import pallas as pl
from jax.experimental.pallas import tpu as pltpu
from jax.sharding import Mesh
from jax.sharding import PartitionSpec as P

AXES = ("x", "zh", "zl", "y", "c")
ROW = ("x", "zh")
COL = ("zl", "y", "c")
CHIPS = ("x", "zh", "zl", "y")
SWAP = [(0, 1), (1, 0)]
STEP_COLS = 10


def share(array, axes):
    devices = lax.axis_size(axes)
    return lax.all_to_all(
        jnp.broadcast_to(array[None], (devices, *array.shape)), axes, 0, 0, tiled=True
    )


def ladder_kernel(core_ref, own_ref, other_ref, ints_ref, amps_ref, res_ref, energy_ref, cols_ref, sum_ref):
    step = pl.program_id(0)
    nb, rows, window = ints_ref.shape

    @pl.when(step == 0)
    def _():
        core = core_ref[0]
        cols_ref[:, core] = own_ref[...]
        cols_ref[:, 1 - core] = other_ref[...]
        sum_ref[...] = jnp.zeros_like(sum_ref)

    pad = -rows % 8
    whole = rows // 8 * 8

    def padded(block):
        if pad == 0:
            return block
        return jnp.concatenate([block, jnp.zeros((pad, window), block.dtype)], 0)

    lhs = jnp.concatenate([padded(ints_ref[j]) for j in range(nb)], 0)
    cols = cols_ref[...].reshape(window, -1)
    full = jnp.dot(lhs, cols, preferred_element_type=jnp.float32)
    for j in range(nb):
        part = full[j * (rows + pad) : j * (rows + pad) + rows]
        res_ref[j] = part.astype(res_ref.dtype)
        product = amps_ref[j].astype(jnp.float32) * part
        sum_ref[...] += jnp.sum(product[:whole].reshape(whole // 8, 8, -1), 0)
        if rows > whole:
            sum_ref[: rows - whole] += product[whole:]

    @pl.when(step == pl.num_programs(0) - 1)
    def _():
        energy_ref[...] = jnp.sum(sum_ref[...], 0, keepdims=True)


def ladder(core, own, other, ints, amps):
    blocks, rows, window = ints.shape
    pairs = amps.shape[2]
    nb = STEP_COLS
    moving = lambda s, c: (s, 0, 0)
    still = lambda s, c: (0, 0, 0)
    return pl.pallas_call(
        ladder_kernel,
        out_shape=(
            jax.ShapeDtypeStruct(amps.shape, jnp.bfloat16),
            jax.ShapeDtypeStruct((1, pairs), jnp.float32),
        ),
        grid_spec=pltpu.PrefetchScalarGridSpec(
            num_scalar_prefetch=1,
            grid=(blocks // nb,),
            in_specs=[
                pl.BlockSpec(own.shape, still),
                pl.BlockSpec(other.shape, still),
                pl.BlockSpec((nb, rows, window), moving),
                pl.BlockSpec((nb, rows, pairs), moving),
            ],
            out_specs=[
                pl.BlockSpec((nb, rows, pairs), moving),
                pl.BlockSpec((1, pairs), lambda s, c: (0, 0)),
            ],
            scratch_shapes=[
                pltpu.VMEM((own.shape[0], 2, own.shape[1], pairs), own.dtype),
                pltpu.VMEM((8, pairs), jnp.float32),
            ],
        ),
        compiler_params=pltpu.CompilerParams(
            vmem_limit_bytes=48 << 20, dimension_semantics=("arbitrary",)
        ),
        cost_estimate=pl.CostEstimate(
            flops=2 * blocks * rows * window * pairs,
            bytes_accessed=2 * blocks * rows * (window + 2 * pairs),
            transcendentals=0,
        ),
    )(core, own, other, ints, amps)


def shards(amplitudes, integrals, window_index):
    block_rows, block_cols, pairs = amplitudes.shape
    window = integrals.shape[2]
    per_device = window // lax.axis_size(AXES)
    row_rank = lax.axis_index(ROW)
    col_rank = lax.axis_index(COL)
    virtuals = block_rows * lax.axis_size(ROW)
    owned_index = lax.dynamic_slice_in_dim(window_index, lax.axis_index(AXES) * per_device, per_device)
    row_offset = owned_index // virtuals - row_rank * block_rows
    col_offset = owned_index % virtuals - col_rank * block_cols
    owned = amplitudes[row_offset, col_offset]
    line = share(owned, ("y",)).reshape(-1, pairs)
    own = share(line, ("x", "zh", "zl")).reshape(-1, per_device, pairs)
    other = lax.ppermute(own, "c", SWAP)
    core = lax.axis_index("c").reshape(1)
    residual, energy = ladder(
        core, own, other, integrals.transpose(1, 0, 2), amplitudes.transpose(1, 0, 2)
    )
    chip = energy + lax.ppermute(energy, "c", SWAP)
    total = jnp.sum(share(chip, CHIPS), axis=(0, 1))
    return residual.transpose(1, 0, 2), total / virtuals


def solution(mesh):
    finer = Mesh(mesh.devices.reshape(4, 2, 2, 4, 2), AXES)
    placed = (P(ROW, COL, None), P(ROW, COL, None), P())
    return jax.shard_map(
        shards, mesh=finer, in_specs=placed, out_specs=(P(ROW, COL, None), P()), check_vma=False
    )
```

```python
import functools

import jax
import jax.numpy as jnp
from jax import lax
from jax.experimental import pallas as pl
from jax.experimental.pallas import tpu as pltpu
from jax.sharding import Mesh
from jax.sharding import PartitionSpec as P

AXES = ("x", "zh", "zl", "y", "c")
ROW = ("x", "zh")
COL = ("zl", "y", "c")
CHIPS = ("x", "zh", "zl", "y")
PLANE = ("zh", "zl", "y")
SWAP = [(0, 1), (1, 0)]
RING = 4
ACROSS = [(x, (x + 2) % RING) for x in range(RING)]
BOTH_WAYS = [(2 * x, 2 * ((x + 1) % RING)) for x in range(RING)] + [
    (2 * x + 1, 2 * ((x - 1) % RING) + 1) for x in range(RING)
]
STEP_COLS = 10
LAST_COLS = 10
FIRST_VMEM = 16 << 20
LAST_VMEM = 24 << 20


def share(array, axes):
    devices = lax.axis_size(axes)
    return lax.all_to_all(
        jnp.broadcast_to(array[None], (devices, *array.shape)), axes, 0, 0, tiled=True
    )


def padded_rows(ref, nb):
    pad = -ref.shape[1] % 8

    def padded(block):
        if pad == 0:
            return block
        return jnp.concatenate([block, jnp.zeros((pad, block.shape[1]), block.dtype)], 0)

    return jnp.concatenate([padded(ref[j]) for j in range(nb)], 0)


def first_kernel(place_ref, mine_ref, theirs_ref, ints_ref, sum_ref, cols_ref):
    chunk, core = place_ref[0], place_ref[1]
    cols_ref[:, core] = mine_ref[...]
    cols_ref[:, 1 - core] = theirs_ref[...]
    blocks, rows, _ = ints_ref.shape
    depth, pairs = cols_ref.shape[0] * 2 * cols_ref.shape[2], cols_ref.shape[3]
    nb = STEP_COLS

    def body(block_ref):
        at = pl.ds(pl.program_id(0) * nb, nb)
        cols = cols_ref[...].reshape(depth, pairs)
        term = jnp.dot(padded_rows(block_ref, nb), cols, preferred_element_type=jnp.float32)
        sum_ref[at] = term.reshape(nb, -1, pairs)

    pltpu.emit_pipeline(
        body,
        grid=(blocks // nb,),
        in_specs=[pl.BlockSpec((nb, rows, depth), lambda s: (s, 0, chunk))],
        out_specs=[],
    )(ints_ref)


def last_kernel(
    place_ref, near_ref, far_ref, o_mine_ref, o_theirs_ref, ints_ref, sum_ref, amps_ref, res_ref, energy_ref, cols_ref, part_ref
):
    chunk, core = place_ref[0], place_ref[1]
    near = lax.rem(chunk + jnp.where(core == 0, RING - 1, 1), RING)
    far = lax.rem(chunk + jnp.where(core == 0, 1, RING - 1), RING)
    across = lax.rem(chunk + 2, RING)
    cols_ref[0, :, core] = near_ref[0]
    cols_ref[0, :, 1 - core] = near_ref[1]
    cols_ref[1, :, 1 - core] = far_ref[0]
    cols_ref[1, :, core] = far_ref[1]
    cols_ref[2, :, core] = o_mine_ref[...]
    cols_ref[2, :, 1 - core] = o_theirs_ref[...]
    part_ref[...] = jnp.zeros_like(part_ref)
    blocks, rows, _ = ints_ref.shape
    depth, pairs = cols_ref.shape[1] * 2 * cols_ref.shape[3], cols_ref.shape[4]
    nb = LAST_COLS
    whole = rows // 8 * 8

    def body(near_ints, far_ints, across_ints, out_ref):
        lhs = jnp.concatenate([padded_rows(r, nb) for r in (near_ints, far_ints, across_ints)], 1)
        cols = cols_ref[...].reshape(3 * depth, pairs)
        term = jnp.dot(lhs, cols, preferred_element_type=jnp.float32).reshape(nb, -1, pairs)
        for j in range(nb):
            at = pl.program_id(0) * nb + j
            full = (sum_ref[at] + term[j])[:rows]
            out_ref[j] = full.astype(jnp.bfloat16)
            product = amps_ref[at].astype(jnp.float32) * full
            part_ref[...] += jnp.sum(product[:whole].reshape(whole // 8, 8, -1), 0)
            if rows > whole:
                part_ref[: rows - whole] += product[whole:]

    pltpu.emit_pipeline(
        body,
        grid=(blocks // nb,),
        in_specs=[
            pl.BlockSpec((nb, rows, depth), lambda s: (s, 0, near)),
            pl.BlockSpec((nb, rows, depth), lambda s: (s, 0, far)),
            pl.BlockSpec((nb, rows, depth), lambda s: (s, 0, across)),
        ],
        out_specs=[pl.BlockSpec((nb, rows, pairs), lambda s: (s, 0, 0))],
    )(ints_ref, ints_ref, ints_ref, res_ref)
    energy_ref[...] = jnp.sum(part_ref[...], 0, keepdims=True)


VMEM_SPEC = pl.BlockSpec(memory_space=pltpu.VMEM)
HBM_SPEC = pl.BlockSpec(memory_space=pltpu.HBM)
SMEM_SPEC = pl.BlockSpec(memory_space=pltpu.SMEM)


def first_chunk(place, mine, theirs, ints):
    blocks, rows, window = ints.shape
    pairs = mine.shape[2]
    depth = window // RING
    return pl.pallas_call(
        first_kernel,
        out_shape=pltpu.VMEM((blocks, rows + -rows % 8, pairs), jnp.float32),
        in_specs=[SMEM_SPEC, VMEM_SPEC, VMEM_SPEC, HBM_SPEC],
        out_specs=VMEM_SPEC,
        scratch_shapes=[pltpu.VMEM((mine.shape[0], 2, *mine.shape[1:]), mine.dtype)],
        compiler_params=pltpu.CompilerParams(vmem_limit_bytes=FIRST_VMEM),
        cost_estimate=pl.CostEstimate(
            flops=2 * blocks * rows * depth * pairs, bytes_accessed=2 * blocks * rows * depth, transcendentals=0
        ),
    )(place, mine, theirs, ints)


def last_chunks(place, near, far, o_mine, o_theirs, ints, total, amps):
    blocks, rows, window = ints.shape
    pairs = amps.shape[2]
    depth = window // RING
    return pl.pallas_call(
        last_kernel,
        out_shape=(
            jax.ShapeDtypeStruct(amps.shape, jnp.bfloat16),
            jax.ShapeDtypeStruct((1, pairs), jnp.float32),
        ),
        in_specs=[SMEM_SPEC, VMEM_SPEC, VMEM_SPEC, VMEM_SPEC, VMEM_SPEC, HBM_SPEC, VMEM_SPEC, VMEM_SPEC],
        out_specs=(HBM_SPEC, VMEM_SPEC),
        scratch_shapes=[
            pltpu.VMEM((RING - 1, o_mine.shape[0], 2, *o_mine.shape[1:]), o_mine.dtype),
            pltpu.VMEM((8, pairs), jnp.float32),
        ],
        compiler_params=pltpu.CompilerParams(vmem_limit_bytes=LAST_VMEM),
        cost_estimate=pl.CostEstimate(
            flops=6 * blocks * rows * depth * pairs,
            bytes_accessed=2 * blocks * rows * (3 * depth + 2 * pairs),
            transcendentals=0,
        ),
    )(place, near, far, o_mine, o_theirs, ints, total, amps)


def shards(amplitudes, integrals, window_index):
    block_rows, block_cols, pairs = amplitudes.shape
    window = integrals.shape[2]
    per_device = window // lax.axis_size(AXES)
    row_rank = lax.axis_index(ROW)
    col_rank = lax.axis_index(COL)
    virtuals = block_rows * lax.axis_size(ROW)
    owned_index = lax.dynamic_slice_in_dim(window_index, lax.axis_index(AXES) * per_device, per_device)
    row_offset = owned_index // virtuals - row_rank * block_rows
    col_offset = owned_index % virtuals - col_rank * block_cols
    owned = amplitudes[row_offset, col_offset]
    ints, amps = integrals.transpose(1, 0, 2), amplitudes.transpose(1, 0, 2)

    ints = pltpu.with_memory_space_constraint(ints, pltpu.HBM)
    place = jnp.stack([lax.axis_index("x"), lax.axis_index("c")])

    mine = share(owned, PLANE)
    theirs = lax.ppermute(mine, "c", SWAP)
    o_mine = lax.ppermute(mine, "x", ACROSS)
    near = lax.ppermute(jnp.stack([mine, theirs]), ("x", "c"), BOTH_WAYS)
    total = first_chunk(place, mine, theirs, ints)
    near, o_mine, total = lax.optimization_barrier((near, o_mine, total))
    o_theirs = lax.ppermute(o_mine, "c", SWAP)
    far = lax.ppermute(near, "c", SWAP)
    residual, energy = last_chunks(place, near, far, o_mine, o_theirs, ints, total, amps)

    chip = energy + lax.ppermute(energy, "c", SWAP)
    total_energy = jnp.sum(share(chip, CHIPS), axis=(0, 1))
    return residual.transpose(1, 0, 2), total_energy / virtuals


def solution(mesh):
    finer = Mesh(mesh.devices.reshape(4, 2, 2, 4, 2), AXES)
    placed = (P(ROW, COL, None), P(ROW, COL, None), P())
    return jax.shard_map(
        shards, mesh=finer, in_specs=placed, out_specs=(P(ROW, COL, None), P()), check_vma=False
    )
```

```python
import functools

import jax
import jax.numpy as jnp
from jax import lax
from jax.experimental import pallas as pl
from jax.experimental.pallas import tpu as pltpu
from jax.sharding import Mesh
from jax.sharding import PartitionSpec as P

AXES = ("x", "zh", "zl", "y", "c")
ROW = ("x", "zh")
COL = ("zl", "y", "c")
CHIPS = ("x", "zh", "zl", "y")
SWAP = [(0, 1), (1, 0)]
RING = 4


def device(x, z, y, core):
    return ((x * RING + z) * RING + y) * 2 + core


def plane_groups():
    ring = range(RING)
    of_x = [[device(x, z, y, 0) for z in ring for y in ring] for x in ring]
    of_z = [[device(x, z, y, 1) for x in ring for y in ring] for z in ring]
    return of_x + of_z


def turned(by):
    ring = range(RING)
    return [
        (device(x, z, y, 0), device((x + by) % RING, z, y, 0)) for x in ring for z in ring for y in ring
    ] + [(device(x, z, y, 1), device(x, (z + by) % RING, y, 1)) for x in ring for z in ring for y in ring]


LAST_COLS = 10
LANES = 256
FETCH_VMEM = 4 << 20
LAST_VMEM = 16 << 20


def share(array, axes, groups=None):
    devices = lax.axis_size(axes) if groups is None else len(groups[0])
    return lax.all_to_all(
        jnp.broadcast_to(array[None], (devices, *array.shape)),
        axes,
        0,
        0,
        axis_index_groups=groups,
        tiled=True,
    )


def padded_rows(ref, nb):
    pad = -ref.shape[1] % 8

    def padded(block):
        if pad == 0:
            return block
        return jnp.concatenate([block, jnp.zeros((pad, block.shape[1]), block.dtype)], 0)

    return jnp.concatenate([padded(ref[j]) for j in range(nb)], 0)


VMEM_SPEC = pl.BlockSpec(memory_space=pltpu.VMEM)
HBM_SPEC = pl.BlockSpec(memory_space=pltpu.HBM)
SMEM_SPEC = pl.BlockSpec(memory_space=pltpu.SMEM)


def fetch_kernel(after_ref, ints_ref, amps_ref, ints_out, amps_out, token_out, sems):
    token_out[...] = after_ref[0]
    copies = [
        pltpu.make_async_copy(ints_ref, ints_out, sems.at[0]),
        pltpu.make_async_copy(amps_ref, amps_out, sems.at[1]),
    ]
    for copy in copies:
        copy.start()
    for copy in copies:
        copy.wait()


def fetch(after, ints, amps):
    return pl.pallas_call(
        fetch_kernel,
        out_shape=tuple(pltpu.VMEM(a.shape, a.dtype) for a in (ints, amps, after[0])),
        in_specs=[VMEM_SPEC, HBM_SPEC, HBM_SPEC],
        out_specs=(VMEM_SPEC, VMEM_SPEC, VMEM_SPEC),
        scratch_shapes=[pltpu.SemaphoreType.DMA((2,))],
        compiler_params=pltpu.CompilerParams(vmem_limit_bytes=FETCH_VMEM),
        cost_estimate=pl.CostEstimate(
            flops=0, bytes_accessed=2 * (ints.size + amps.size), transcendentals=0
        ),
    )(after, *(pltpu.with_memory_space_constraint(a, pltpu.HBM) for a in (ints, amps)))


def ladder_kernel(place_ref, *refs):
    mine, theirs = refs[:RING], refs[RING : 2 * RING]
    ints_ref, amps_ref, _, res_ref, energy_ref, cols_ref, part_ref = refs[2 * RING :]
    x, z, core = place_ref[0], place_ref[1], place_ref[2]
    pairs = amps_ref.shape[2]

    def put(of_core_0, of_core_1):
        for turn in range(RING):
            plane = (RING, RING, *of_core_0[turn].shape[1:])
            cols_ref[lax.rem(x + turn, RING), :, :, 0] = of_core_0[turn][...].reshape(plane)
            cols_ref[:, lax.rem(z + turn, RING), :, 1] = of_core_1[turn][...].reshape(plane)

    @pl.when(core == 0)
    def _():
        put(mine, theirs)

    @pl.when(core != 0)
    def _():
        put(theirs, mine)

    part_ref[...] = jnp.zeros_like(part_ref)
    blocks, rows, window = ints_ref.shape
    nb = LAST_COLS
    whole = rows // 8 * 8

    def body(out_ref):
        start = pl.program_id(0) * nb
        lhs = padded_rows(ints_ref.at[pl.ds(start, nb)], nb)
        cols = cols_ref[...].reshape(window, pairs)
        for at in range(0, pairs, LANES):
            cut = slice(at, at + LANES)
            total = jnp.dot(lhs, cols[:, cut], preferred_element_type=jnp.float32)
            total = total.reshape(nb, -1, LANES)
            for j in range(nb):
                full = total[j, :rows]
                out_ref[j, :, cut] = full.astype(jnp.bfloat16)
                product = amps_ref[start + j, :, cut].astype(jnp.float32) * full
                part_ref[:, cut] += jnp.sum(product[:whole].reshape(whole // 8, 8, -1), 0)
                if rows > whole:
                    part_ref[: rows - whole, cut] += product[whole:]

    pltpu.emit_pipeline(
        body,
        grid=(blocks // nb,),
        in_specs=[],
        out_specs=[pl.BlockSpec((nb, rows, pairs), lambda s: (s, 0, 0))],
    )(res_ref)
    energy_ref[...] = jnp.sum(part_ref[...], 0, keepdims=True)


def ladder(place, mine, theirs, ints, amps, token):
    blocks, rows, window = ints.shape
    pairs = amps.shape[2]
    return pl.pallas_call(
        ladder_kernel,
        out_shape=(
            jax.ShapeDtypeStruct(amps.shape, jnp.bfloat16),
            jax.ShapeDtypeStruct((1, pairs), jnp.float32),
        ),
        in_specs=[SMEM_SPEC] + [VMEM_SPEC] * (2 * RING + 3),
        out_specs=(HBM_SPEC, VMEM_SPEC),
        scratch_shapes=[
            pltpu.VMEM((RING, RING, RING, 2, *mine[0].shape[1:]), mine[0].dtype),
            pltpu.VMEM((8, pairs), jnp.float32),
        ],
        compiler_params=pltpu.CompilerParams(vmem_limit_bytes=LAST_VMEM),
        cost_estimate=pl.CostEstimate(
            flops=2 * blocks * rows * window * pairs,
            bytes_accessed=2 * blocks * rows * (window + 2 * pairs),
            transcendentals=0,
        ),
    )(place, *mine, *theirs, ints, amps, token)


def shards(amplitudes, integrals, window_index):
    block_rows, block_cols, pairs = amplitudes.shape
    window = integrals.shape[2]
    per_device = window // lax.axis_size(AXES)
    row_rank = lax.axis_index(ROW)
    col_rank = lax.axis_index(COL)
    virtuals = block_rows * lax.axis_size(ROW)
    owned_index = lax.dynamic_slice_in_dim(window_index, lax.axis_index(AXES) * per_device, per_device)
    row_offset = owned_index // virtuals - row_rank * block_rows
    col_offset = owned_index % virtuals - col_rank * block_cols
    owned = amplitudes[row_offset, col_offset]
    ints, amps = integrals.transpose(1, 0, 2), amplitudes.transpose(1, 0, 2)
    place = jnp.stack([lax.axis_index("x"), lax.axis_index(("zh", "zl")), lax.axis_index("c")])

    owned, place = lax.optimization_barrier((owned, place))
    plane = share(owned, AXES, plane_groups())
    swapped = lambda array: lax.ppermute(array, "c", SWAP)
    across = lax.ppermute(plane, AXES, turned(2))
    above = lax.ppermute(plane, AXES, turned(-1))
    below = lax.ppermute(plane, AXES, turned(1))
    there = swapped(plane)
    ints, amps, token = fetch(there, ints, amps)
    above, across, below, token = lax.optimization_barrier((above, across, below, token))
    mine = (plane, above, across, below)
    theirs = (there, swapped(above), swapped(across), swapped(below))
    residual, energy = ladder(place, mine, theirs, ints, amps, token)

    chip = energy + lax.ppermute(energy, "c", SWAP)
    total_energy = jnp.sum(share(chip, CHIPS), axis=(0, 1))
    return residual.transpose(1, 0, 2), total_energy / virtuals


def solution(mesh):
    finer = Mesh(mesh.devices.reshape(4, 2, 2, 4, 2), AXES)
    placed = (P(ROW, COL, None), P(ROW, COL, None), P())
    return jax.shard_map(
        shards, mesh=finer, in_specs=placed, out_specs=(P(ROW, COL, None), P()), check_vma=False
    )
```

```python
import functools

import jax
import jax.numpy as jnp
from jax import lax
from jax.experimental import pallas as pl
from jax.experimental.pallas import tpu as pltpu
from jax.sharding import Mesh
from jax.sharding import PartitionSpec as P

AXES = ("x", "zh", "zl", "y", "c")
ROW = ("x", "zh")
COL = ("zl", "y", "c")
CHIPS = ("x", "zh", "zl", "y")
SWAP = [(0, 1), (1, 0)]
RING = 4


def device(x, z, y, core):
    return ((x * RING + z) * RING + y) * 2 + core


def plane_groups():
    ring = range(RING)
    of_x = [[device(x, z, y, 0) for z in ring for y in ring] for x in ring]
    of_z = [[device(x, z, y, 1) for x in ring for y in ring] for z in ring]
    return of_x + of_z


def turned(by):
    ring = range(RING)
    return [
        (device(x, z, y, 0), device((x + by) % RING, z, y, 0)) for x in ring for z in ring for y in ring
    ] + [(device(x, z, y, 1), device(x, (z + by) % RING, y, 1)) for x in ring for z in ring for y in ring]


LAST_COLS = 10
LANES = 256
EARLY = 30
FETCH_VMEM = 24 << 20
SPREAD_VMEM = 2 << 20
LAST_VMEM = 16 << 20


def share(array, axes, groups=None):
    devices = lax.axis_size(axes) if groups is None else len(groups[0])
    return lax.all_to_all(
        jnp.broadcast_to(array[None], (devices, *array.shape)),
        axes,
        0,
        0,
        axis_index_groups=groups,
        tiled=True,
    )


def padded_rows(ref, nb):
    pad = -ref.shape[1] % 8

    def padded(block):
        if pad == 0:
            return block
        return jnp.concatenate([block, jnp.zeros((pad, block.shape[1]), block.dtype)], 0)

    return jnp.concatenate([padded(ref[j]) for j in range(nb)], 0)


VMEM_SPEC = pl.BlockSpec(memory_space=pltpu.VMEM)
HBM_SPEC = pl.BlockSpec(memory_space=pltpu.HBM)
SMEM_SPEC = pl.BlockSpec(memory_space=pltpu.SMEM)


def fetch_kernel(
    after_ref, ints_ref, amps_ref, early_ints, early_amps, weights_out, token_out, late_ints, late_amps, sems
):
    blocks = ints_ref.shape[0]
    late, early = pl.ds(EARLY, blocks - EARLY), pl.ds(0, EARLY)
    copies = [
        pltpu.make_async_copy(ints_ref.at[late], late_ints, sems.at[0]),
        pltpu.make_async_copy(amps_ref.at[late], late_amps, sems.at[1]),
        pltpu.make_async_copy(ints_ref.at[early], early_ints, sems.at[2]),
        pltpu.make_async_copy(amps_ref.at[early], early_amps, sems.at[3]),
    ]
    for copy in copies:
        copy.start()
    token_out[...] = after_ref[0]
    copies[0].wait()
    copies[1].wait()
    for n in range((blocks - EARLY) // LAST_COLS):
        span = pl.ds(n * LAST_COLS, LAST_COLS)
        term = lax.dot_general(
            padded_rows(late_ints.at[span], LAST_COLS),
            padded_rows(late_amps.at[span], LAST_COLS),
            (((0,), (0,)), ((), ())),
            preferred_element_type=jnp.float32,
        )
        weights_out[...] = term if n == 0 else weights_out[...] + term
    copies[2].wait()
    copies[3].wait()


def fetch(after, ints, amps):
    late = ints.shape[0] - EARLY
    kept = (
        pltpu.VMEM((EARLY, *ints.shape[1:]), ints.dtype),
        pltpu.VMEM((EARLY, *amps.shape[1:]), amps.dtype),
    )
    return pl.pallas_call(
        fetch_kernel,
        out_shape=kept
        + (pltpu.VMEM((ints.shape[2], amps.shape[2]), jnp.float32), pltpu.VMEM(after.shape[1:], after.dtype)),
        in_specs=[VMEM_SPEC, HBM_SPEC, HBM_SPEC],
        out_specs=(VMEM_SPEC,) * 4,
        scratch_shapes=[
            pltpu.VMEM((late, *ints.shape[1:]), ints.dtype),
            pltpu.VMEM((late, *amps.shape[1:]), amps.dtype),
            pltpu.SemaphoreType.DMA((4,)),
        ],
        compiler_params=pltpu.CompilerParams(vmem_limit_bytes=FETCH_VMEM),
        cost_estimate=pl.CostEstimate(
            flops=2 * late * ints.shape[1] * ints.shape[2] * amps.shape[2],
            bytes_accessed=2 * (ints.size + amps.size),
            transcendentals=0,
        ),
    )(after, ints, amps)


def columns_times(ints_ref, cols_ref, start, nb, done):
    window, pairs = ints_ref.shape[2], cols_ref.shape[-1]
    lhs = padded_rows(ints_ref.at[pl.ds(start, nb)], nb)
    cols = cols_ref[...].reshape(window, pairs)
    for at in range(0, pairs, LANES):
        cut = slice(at, at + LANES)
        total = jnp.dot(lhs, cols[:, cut], preferred_element_type=jnp.float32)
        done(cut, total.reshape(nb, -1, LANES))


def early_kernel(place_ref, *refs):
    mine, theirs = refs[:RING], refs[RING : 2 * RING]
    ints_ref, amps_ref, weights_ref, _ = refs[2 * RING : 2 * RING + 4]
    res_ref, energy_ref, cols_ref, part_ref = refs[2 * RING + 4 :]
    x, z, core = place_ref[0], place_ref[1], place_ref[2]
    _, rows, window = ints_ref.shape
    pairs = amps_ref.shape[2]
    nb = LAST_COLS
    whole = rows // 8 * 8

    def put(of_core_0, of_core_1):
        for turn in range(RING):
            plane = (RING, RING, *of_core_0[turn].shape[1:])
            cols_ref[lax.rem(x + turn, RING), :, :, 0] = of_core_0[turn][...].reshape(plane)
            cols_ref[:, lax.rem(z + turn, RING), :, 1] = of_core_1[turn][...].reshape(plane)

    @pl.when(core == 0)
    def _():
        put(mine, theirs)

    @pl.when(core != 0)
    def _():
        put(theirs, mine)

    part_ref[...] = jnp.zeros_like(part_ref)
    per_x = window // RING
    for at in range(RING):
        of_x = cols_ref[at].reshape(per_x, pairs).astype(jnp.float32)
        product = of_x * weights_ref[at * per_x : (at + 1) * per_x]
        part_ref[...] += jnp.sum(product.reshape(per_x // 8, 8, pairs), 0)

    def body(out_ref):
        start = pl.program_id(0) * nb

        def done(cut, total):
            for j in range(nb):
                full = total[j, :rows]
                out_ref[j, :, cut] = full.astype(jnp.bfloat16)
                product = amps_ref[start + j, :, cut].astype(jnp.float32) * full
                part_ref[:, cut] += jnp.sum(product[:whole].reshape(whole // 8, 8, -1), 0)
                if rows > whole:
                    part_ref[: rows - whole, cut] += product[whole:]

        columns_times(ints_ref, cols_ref, start, nb, done)

    pltpu.emit_pipeline(
        body,
        grid=(EARLY // nb,),
        in_specs=[],
        out_specs=[pl.BlockSpec((nb, rows, pairs), lambda s: (s, 0, 0))],
    )(res_ref)
    energy_ref[...] = jnp.sum(part_ref[...], 0, keepdims=True)


def late_kernel(cols_ref, ints_ref, _, res_ref):
    blocks, rows, window = ints_ref.shape
    nb = LAST_COLS
    first = EARLY // nb

    def body(block_ref, out_ref):
        def done(cut, total):
            for j in range(nb):
                out_ref[j, :, cut] = total[j, :rows].astype(jnp.bfloat16)

        columns_times(block_ref, cols_ref, 0, nb, done)

    pltpu.emit_pipeline(
        body,
        grid=((blocks - EARLY) // nb,),
        in_specs=[pl.BlockSpec((nb, rows, window), lambda s: (s + first, 0, 0))],
        out_specs=[pl.BlockSpec((nb, rows, cols_ref.shape[-1]), lambda s: (s + first, 0, 0))],
    )(ints_ref, res_ref)


def early_columns(place, mine, theirs, ints, amps, weights, token, blocks):
    _, rows, window = ints.shape
    pairs = amps.shape[2]
    return pl.pallas_call(
        early_kernel,
        out_shape=(
            jax.ShapeDtypeStruct((blocks, *amps.shape[1:]), jnp.bfloat16),
            pltpu.VMEM((1, pairs), jnp.float32),
            pltpu.VMEM((RING, RING, RING, 2, *mine[0].shape[1:]), mine[0].dtype),
        ),
        in_specs=[SMEM_SPEC] + [VMEM_SPEC] * (2 * RING + 4),
        out_specs=(HBM_SPEC, VMEM_SPEC, VMEM_SPEC),
        scratch_shapes=[pltpu.VMEM((8, pairs), jnp.float32)],
        compiler_params=pltpu.CompilerParams(vmem_limit_bytes=LAST_VMEM),
        cost_estimate=pl.CostEstimate(
            flops=2 * EARLY * rows * window * pairs, bytes_accessed=2 * EARLY * rows * pairs, transcendentals=0
        ),
    )(place, *mine, *theirs, ints, amps, weights, token)


def late_columns(cols, ints, residual):
    blocks, rows, window = ints.shape
    pairs = residual.shape[2]
    late = blocks - EARLY
    return pl.pallas_call(
        late_kernel,
        out_shape=jax.ShapeDtypeStruct(residual.shape, residual.dtype),
        in_specs=[VMEM_SPEC, HBM_SPEC, HBM_SPEC],
        out_specs=HBM_SPEC,
        input_output_aliases={2: 0},
        compiler_params=pltpu.CompilerParams(vmem_limit_bytes=LAST_VMEM),
        cost_estimate=pl.CostEstimate(
            flops=2 * late * rows * window * pairs,
            bytes_accessed=2 * late * rows * (window + pairs),
            transcendentals=0,
        ),
    )(cols, ints, residual)


def spread_kernel(mine_ref, theirs_ref, out_ref):
    out_ref[...] = jnp.broadcast_to((mine_ref[...] + theirs_ref[...])[None], out_ref.shape)


def spread(mine, theirs, copies):
    return pl.pallas_call(
        spread_kernel,
        out_shape=jax.ShapeDtypeStruct((copies, *mine.shape), mine.dtype),
        in_specs=[VMEM_SPEC, VMEM_SPEC],
        out_specs=VMEM_SPEC,
        compiler_params=pltpu.CompilerParams(vmem_limit_bytes=SPREAD_VMEM),
    )(mine, theirs)


def shards(amplitudes, integrals, window_index):
    block_rows, block_cols, pairs = amplitudes.shape
    window = integrals.shape[2]
    per_device = window // lax.axis_size(AXES)
    row_rank = lax.axis_index(ROW)
    col_rank = lax.axis_index(COL)
    virtuals = block_rows * lax.axis_size(ROW)
    owned_index = lax.dynamic_slice_in_dim(window_index, lax.axis_index(AXES) * per_device, per_device)
    row_offset = owned_index // virtuals - row_rank * block_rows
    col_offset = owned_index % virtuals - col_rank * block_cols
    owned = amplitudes[row_offset, col_offset]
    ints, amps = integrals.transpose(1, 0, 2), amplitudes.transpose(1, 0, 2)
    place = jnp.stack([lax.axis_index("x"), lax.axis_index(("zh", "zl")), lax.axis_index("c")])

    owned, place = lax.optimization_barrier((owned, place))
    plane = share(owned, AXES, plane_groups())
    swapped = lambda array: lax.ppermute(array, "c", SWAP)
    across = lax.ppermute(plane, AXES, turned(2))
    above = lax.ppermute(plane, AXES, turned(-1))
    below = lax.ppermute(plane, AXES, turned(1))
    there = swapped(plane)
    ints, amps = (pltpu.with_memory_space_constraint(a, pltpu.HBM) for a in (ints, amps))
    early_ints, early_amps, weights, token = fetch(there, ints, amps)
    above, across, below, token = lax.optimization_barrier((above, across, below, token))
    mine = (plane, above, across, below)
    theirs = (there, swapped(above), swapped(across), swapped(below))
    residual, energy, cols = early_columns(
        place, mine, theirs, early_ints, early_amps, weights, token, block_cols
    )

    chips = spread(energy, swapped(energy), lax.axis_size(CHIPS))
    total_energy = jnp.sum(lax.all_to_all(chips, CHIPS, 0, 0, tiled=True), axis=(0, 1))
    residual = late_columns(cols, ints, residual)
    return residual.transpose(1, 0, 2), total_energy / virtuals


def solution(mesh):
    finer = Mesh(mesh.devices.reshape(4, 2, 2, 4, 2), AXES)
    placed = (P(ROW, COL, None), P(ROW, COL, None), P())
    return jax.shard_map(
        shards, mesh=finer, in_specs=placed, out_specs=(P(ROW, COL, None), P()), check_vma=False
    )
```

```python
import functools

import jax
import jax.numpy as jnp
from jax import lax
from jax.experimental import pallas as pl
from jax.experimental.pallas import tpu as pltpu
from jax.sharding import Mesh
from jax.sharding import PartitionSpec as P

AXES = ("x", "zh", "zl", "y", "c")
ROW = ("x", "zh")
COL = ("zl", "y", "c")
CHIPS = ("x", "zh", "zl", "y")
SWAP = [(0, 1), (1, 0)]
RING = 4


def device(x, z, y, core):
    return ((x * RING + z) * RING + y) * 2 + core


def plane_groups():
    ring = range(RING)
    of_x = [[device(x, z, y, 0) for z in ring for y in ring] for x in ring]
    of_z = [[device(x, z, y, 1) for x in ring for y in ring] for z in ring]
    return of_x + of_z


def turned(by):
    ring = range(RING)
    return [
        (device(x, z, y, 0), device((x + by) % RING, z, y, 0)) for x in ring for z in ring for y in ring
    ] + [(device(x, z, y, 1), device(x, (z + by) % RING, y, 1)) for x in ring for z in ring for y in ring]


LAST_COLS = 10
LANES = 768
EARLY = 30
FETCH_VMEM = 24 << 20
SPREAD_VMEM = 2 << 20
LAST_VMEM = 16 << 20


def share(array, axes, groups=None):
    devices = lax.axis_size(axes) if groups is None else len(groups[0])
    return lax.all_to_all(
        jnp.broadcast_to(array[None], (devices, *array.shape)),
        axes,
        0,
        0,
        axis_index_groups=groups,
        tiled=True,
    )


def padded_rows(ref, nb):
    pad = -ref.shape[1] % 8

    def padded(block):
        if pad == 0:
            return block
        return jnp.concatenate([block, jnp.zeros((pad, block.shape[1]), block.dtype)], 0)

    return jnp.concatenate([padded(ref[j]) for j in range(nb)], 0)


VMEM_SPEC = pl.BlockSpec(memory_space=pltpu.VMEM)
HBM_SPEC = pl.BlockSpec(memory_space=pltpu.HBM)
SMEM_SPEC = pl.BlockSpec(memory_space=pltpu.SMEM)


def fetch_kernel(
    after_ref, ints_ref, amps_ref, early_ints, early_amps, weights_out, token_out, late_ints, late_amps, sems
):
    blocks = ints_ref.shape[0]
    late, early = pl.ds(EARLY, blocks - EARLY), pl.ds(0, EARLY)
    copies = [
        pltpu.make_async_copy(ints_ref.at[late], late_ints, sems.at[0]),
        pltpu.make_async_copy(amps_ref.at[late], late_amps, sems.at[1]),
        pltpu.make_async_copy(ints_ref.at[early], early_ints, sems.at[2]),
        pltpu.make_async_copy(amps_ref.at[early], early_amps, sems.at[3]),
    ]
    for copy in copies:
        copy.start()
    token_out[...] = after_ref[0]
    copies[0].wait()
    copies[1].wait()
    for n in range((blocks - EARLY) // LAST_COLS):
        span = pl.ds(n * LAST_COLS, LAST_COLS)
        term = lax.dot_general(
            padded_rows(late_ints.at[span], LAST_COLS),
            padded_rows(late_amps.at[span], LAST_COLS),
            (((0,), (0,)), ((), ())),
            preferred_element_type=jnp.float32,
        )
        weights_out[...] = term if n == 0 else weights_out[...] + term
    copies[2].wait()
    copies[3].wait()


def fetch(after, ints, amps):
    late = ints.shape[0] - EARLY
    kept = (
        pltpu.VMEM((EARLY, *ints.shape[1:]), ints.dtype),
        pltpu.VMEM((EARLY, *amps.shape[1:]), amps.dtype),
    )
    return pl.pallas_call(
        fetch_kernel,
        out_shape=kept
        + (pltpu.VMEM((ints.shape[2], amps.shape[2]), jnp.float32), pltpu.VMEM(after.shape[1:], after.dtype)),
        in_specs=[VMEM_SPEC, HBM_SPEC, HBM_SPEC],
        out_specs=(VMEM_SPEC,) * 4,
        scratch_shapes=[
            pltpu.VMEM((late, *ints.shape[1:]), ints.dtype),
            pltpu.VMEM((late, *amps.shape[1:]), amps.dtype),
            pltpu.SemaphoreType.DMA((4,)),
        ],
        compiler_params=pltpu.CompilerParams(vmem_limit_bytes=FETCH_VMEM),
        cost_estimate=pl.CostEstimate(
            flops=2 * late * ints.shape[1] * ints.shape[2] * amps.shape[2],
            bytes_accessed=2 * (ints.size + amps.size),
            transcendentals=0,
        ),
    )(after, ints, amps)


def columns_times(ints_ref, cols_ref, start, nb, done):
    window, pairs = ints_ref.shape[2], cols_ref.shape[-1]
    lhs = padded_rows(ints_ref.at[pl.ds(start, nb)], nb)
    cols = cols_ref[...].reshape(window, pairs)
    for at in range(0, pairs, LANES):
        cut = slice(at, at + LANES)
        total = jnp.dot(lhs, cols[:, cut], preferred_element_type=jnp.float32)
        done(cut, total.reshape(nb, -1, LANES))


def early_kernel(place_ref, *refs):
    mine, theirs = refs[:RING], refs[RING : 2 * RING]
    ints_ref, amps_ref, weights_ref, _ = refs[2 * RING : 2 * RING + 4]
    res_ref, energy_ref, cols_ref, part_ref = refs[2 * RING + 4 :]
    x, z, core = place_ref[0], place_ref[1], place_ref[2]
    _, rows, window = ints_ref.shape
    pairs = amps_ref.shape[2]
    nb = LAST_COLS
    whole = rows // 8 * 8

    def put(of_core_0, of_core_1):
        for turn in range(RING):
            plane = (RING, RING, *of_core_0[turn].shape[1:])
            cols_ref[lax.rem(x + turn, RING), :, :, 0] = of_core_0[turn][...].reshape(plane)
            cols_ref[:, lax.rem(z + turn, RING), :, 1] = of_core_1[turn][...].reshape(plane)

    @pl.when(core == 0)
    def _():
        put(mine, theirs)

    @pl.when(core != 0)
    def _():
        put(theirs, mine)

    part_ref[...] = jnp.zeros_like(part_ref)
    per_x = window // RING
    for at in range(RING):
        of_x = cols_ref[at].reshape(per_x, pairs).astype(jnp.float32)
        product = of_x * weights_ref[at * per_x : (at + 1) * per_x]
        part_ref[...] += jnp.sum(product.reshape(per_x // 8, 8, pairs), 0)

    def body(out_ref):
        start = pl.program_id(0) * nb

        def done(cut, total):
            for j in range(nb):
                full = total[j, :rows]
                out_ref[j, :, cut] = full.astype(jnp.bfloat16)
                product = amps_ref[start + j, :, cut].astype(jnp.float32) * full
                part_ref[:, cut] += jnp.sum(product[:whole].reshape(whole // 8, 8, -1), 0)
                if rows > whole:
                    part_ref[: rows - whole, cut] += product[whole:]

        columns_times(ints_ref, cols_ref, start, nb, done)

    pltpu.emit_pipeline(
        body,
        grid=(EARLY // nb,),
        in_specs=[],
        out_specs=[pl.BlockSpec((nb, rows, pairs), lambda s: (s, 0, 0))],
    )(res_ref)
    energy_ref[...] = jnp.sum(part_ref[...], 0, keepdims=True)


def late_kernel(cols_ref, ints_ref, _, res_ref):
    blocks, rows, window = ints_ref.shape
    nb = LAST_COLS
    first = EARLY // nb

    def body(block_ref, out_ref):
        def done(cut, total):
            for j in range(nb):
                out_ref[j, :, cut] = total[j, :rows].astype(jnp.bfloat16)

        columns_times(block_ref, cols_ref, 0, nb, done)

    pltpu.emit_pipeline(
        body,
        grid=((blocks - EARLY) // nb,),
        in_specs=[pl.BlockSpec((nb, rows, window), lambda s: (s + first, 0, 0))],
        out_specs=[pl.BlockSpec((nb, rows, cols_ref.shape[-1]), lambda s: (s + first, 0, 0))],
    )(ints_ref, res_ref)


def early_columns(place, mine, theirs, ints, amps, weights, token, blocks):
    _, rows, window = ints.shape
    pairs = amps.shape[2]
    return pl.pallas_call(
        early_kernel,
        out_shape=(
            jax.ShapeDtypeStruct((blocks, *amps.shape[1:]), jnp.bfloat16),
            pltpu.VMEM((1, pairs), jnp.float32),
            pltpu.VMEM((RING, RING, RING, 2, *mine[0].shape[1:]), mine[0].dtype),
        ),
        in_specs=[SMEM_SPEC] + [VMEM_SPEC] * (2 * RING + 4),
        out_specs=(HBM_SPEC, VMEM_SPEC, VMEM_SPEC),
        scratch_shapes=[pltpu.VMEM((8, pairs), jnp.float32)],
        compiler_params=pltpu.CompilerParams(vmem_limit_bytes=LAST_VMEM),
        cost_estimate=pl.CostEstimate(
            flops=2 * EARLY * rows * window * pairs, bytes_accessed=2 * EARLY * rows * pairs, transcendentals=0
        ),
    )(place, *mine, *theirs, ints, amps, weights, token)


def late_columns(cols, ints, residual):
    blocks, rows, window = ints.shape
    pairs = residual.shape[2]
    late = blocks - EARLY
    return pl.pallas_call(
        late_kernel,
        out_shape=jax.ShapeDtypeStruct(residual.shape, residual.dtype),
        in_specs=[VMEM_SPEC, HBM_SPEC, HBM_SPEC],
        out_specs=HBM_SPEC,
        input_output_aliases={2: 0},
        compiler_params=pltpu.CompilerParams(vmem_limit_bytes=LAST_VMEM),
        cost_estimate=pl.CostEstimate(
            flops=2 * late * rows * window * pairs,
            bytes_accessed=2 * late * rows * (window + pairs),
            transcendentals=0,
        ),
    )(cols, ints, residual)


def spread_kernel(mine_ref, theirs_ref, out_ref):
    out_ref[...] = jnp.broadcast_to((mine_ref[...] + theirs_ref[...])[None], out_ref.shape)


def spread(mine, theirs, copies):
    return pl.pallas_call(
        spread_kernel,
        out_shape=jax.ShapeDtypeStruct((copies, *mine.shape), mine.dtype),
        in_specs=[VMEM_SPEC, VMEM_SPEC],
        out_specs=VMEM_SPEC,
        compiler_params=pltpu.CompilerParams(vmem_limit_bytes=SPREAD_VMEM),
    )(mine, theirs)


def shards(amplitudes, integrals, window_index):
    block_rows, block_cols, pairs = amplitudes.shape
    window = integrals.shape[2]
    per_device = window // lax.axis_size(AXES)
    row_rank = lax.axis_index(ROW)
    col_rank = lax.axis_index(COL)
    virtuals = block_rows * lax.axis_size(ROW)
    owned_index = lax.dynamic_slice_in_dim(window_index, lax.axis_index(AXES) * per_device, per_device)
    row_offset = owned_index // virtuals - row_rank * block_rows
    col_offset = owned_index % virtuals - col_rank * block_cols
    owned = amplitudes[row_offset, col_offset]
    ints, amps = integrals.transpose(1, 0, 2), amplitudes.transpose(1, 0, 2)
    place = jnp.stack([lax.axis_index("x"), lax.axis_index(("zh", "zl")), lax.axis_index("c")])

    owned, place = lax.optimization_barrier((owned, place))
    plane = share(owned, AXES, plane_groups())
    swapped = lambda array: lax.ppermute(array, "c", SWAP)
    across = lax.ppermute(plane, AXES, turned(2))
    above = lax.ppermute(plane, AXES, turned(-1))
    below = lax.ppermute(plane, AXES, turned(1))
    there = swapped(plane)
    ints, amps = (pltpu.with_memory_space_constraint(a, pltpu.HBM) for a in (ints, amps))
    early_ints, early_amps, weights, token = fetch(there, ints, amps)
    above, across, below, token = lax.optimization_barrier((above, across, below, token))
    mine = (plane, above, across, below)
    theirs = (there, swapped(above), swapped(across), swapped(below))
    residual, energy, cols = early_columns(
        place, mine, theirs, early_ints, early_amps, weights, token, block_cols
    )

    chips = spread(energy, swapped(energy), lax.axis_size(CHIPS))
    total_energy = jnp.sum(lax.all_to_all(chips, CHIPS, 0, 0, tiled=True), axis=(0, 1))
    residual = late_columns(cols, ints, residual)
    return residual.transpose(1, 0, 2), total_energy / virtuals


def solution(mesh):
    finer = Mesh(mesh.devices.reshape(4, 2, 2, 4, 2), AXES)
    placed = (P(ROW, COL, None), P(ROW, COL, None), P())
    return jax.shard_map(
        shards, mesh=finer, in_specs=placed, out_specs=(P(ROW, COL, None), P()), check_vma=False
    )
```
